32 devices in a mesh: row: 4 (over z), col: 4 (over y, x), feat: 2 (over core).
Axes of the slice: x: 2, y: 2, z: 4, core: 2. Of those that a mesh axis runs over, the one named last changes fastest.
Arguments:
- tile_values: bfloat16 [4, 4, 80, 128, 128], P('row', 'col')
- tile_rows: int32 [4, 4, 80], P('row', 'col'), may hold values from 0 to 15, as said below
- tile_cols: int32 [4, 4, 80], P('row', 'col'), may hold values from 0 to 15
- tile_mask: int32 [4, 4, 80], P('row', 'col'), may hold values from 0 to 1, as said below
- degree_caps: int32 [8192], P(('row', 'col')), may hold values from 1 to 32, as said below
- clip_groups: int32 [8192], P(('row', 'col')), may hold values from 0 to 7
- clip_bounds: float32 [8], replicated, may hold values from 51.2 to 256
- features: bfloat16 [8192, 256], P('col', 'feat')
- weight: bfloat16 [256, 256], replicated, may hold values from -0.375 to 0.375
- out_grad: bfloat16 [8192, 256], P(('row', 'col'), 'feat')
- dp_noise: float32 [256, 256], P(None, 'feat'), may hold values from -6 to 6
Outputs:
- out_feat: bfloat16 [8192, 256], P(('row', 'col'), 'feat')
- grad_weight: float32 [256, 256], P(None, 'feat')
- grad_input: bfloat16 [8192, 256], P('col', 'feat')
The draws below stay inside these ranges and needn't reach their ends.
Inputs may be any that keep to these rules, and one draw needn't show every extreme that they name: `tile_rows`: each tile slot of one pair of row and col indices names a distinct pair of block row and block column. `tile_mask`: at most all 80 slots of one pair of row and col indices are live; in every draw some pair has all of them live. degree_caps[i] is the number of nonzero entries in row i of A, raised to 1 where it is 0 and capped at 32.
All inputs are finite; a program needn't handle non-finite values.
Results may differ from the reference program's by a relative error of at most 0.006.
Values may be sent and summed in bfloat16 or wider, within the bound.
A program may use at most 128 MiB of HBM per device.

```python
import math
import jax
import jax.numpy as jnp
from jax import lax

BLK = 128
HID = 256
NODE_DEV = 512
TILE_ROW = 5
GROUPS = 8
NODES = 8192
RBLK = 16
CBLK = 16
TPD = 80
N_ROW = 4
N_COL = 4


def tile_layout(key):
    key = jax.random.fold_in(key, 7)
    key_score, key_shuffle, key_rank, key_light = jax.random.split(key, 4)
    pairs = RBLK * CBLK
    slot_total = TPD
    pair_ids = jnp.arange(pairs, dtype=jnp.int32)
    pair_row = pair_ids // CBLK
    pair_col = pair_ids % CBLK
    dev_row = jnp.arange(N_ROW, dtype=jnp.int32)[:, None, None]
    dev_col = jnp.arange(N_COL, dtype=jnp.int32)[None, :, None]
    distance = jnp.abs(dev_row * RBLK + pair_row - dev_col * CBLK - pair_col)
    score = jax.random.randint(key_score, (N_ROW, N_COL, pairs), 0, 2 * CBLK) + jnp.minimum(distance, 2 * CBLK)
    unique = score * pairs + pair_ids
    _, picked = lax.top_k(-unique, slot_total)
    slot_ids = jnp.arange(slot_total, dtype=jnp.int32)
    shuffle_keys = jax.random.randint(key_shuffle, (N_ROW, N_COL, slot_total), 0, 1 << 20) * slot_total + slot_ids
    shuffle = jnp.argsort(shuffle_keys, axis=-1, stable=True)
    picked = jnp.take_along_axis(picked, shuffle, axis=-1)
    rank_keys = jax.random.randint(key_rank, (N_ROW, N_COL, slot_total), 0, 1 << 20) * slot_total + slot_ids
    rank = jnp.argsort(jnp.argsort(rank_keys, axis=-1, stable=True), axis=-1, stable=True)
    heavy = (dev_row * RBLK < (dev_col + 1) * CBLK) & (dev_col * CBLK < (dev_row + 1) * RBLK)
    light = jax.random.randint(key_light, (N_ROW, N_COL, 1), slot_total // 5, slot_total // 2 + 1)
    live_count = jnp.where(heavy, slot_total, light)
    mask_out = (rank < live_count).astype(jnp.int32)
    return ((picked // CBLK).astype(jnp.int32), (picked % CBLK).astype(jnp.int32), mask_out)


def tile_keep(key):
    key_keep = jax.random.fold_in(key, 11)
    rate = max(1, TILE_ROW * N_COL * BLK // 48)
    shape = (N_ROW, N_COL, TPD, BLK, BLK)
    return jax.random.randint(key_keep, shape, 0, rate) == 0


def draw_tile_rows(key, part):
    return tile_layout(key)[0]


def draw_tile_cols(key, part):
    return tile_layout(key)[1]


def draw_tile_mask(key, part):
    return tile_layout(key)[2]


def draw_tile_values(key, part):
    keep = tile_keep(key).astype(jnp.float32)
    key_value = jax.random.fold_in(key, 19)
    shape = (N_ROW, N_COL, TPD, BLK, BLK)
    values = jax.random.normal(key_value, shape, jnp.float32)
    return (values * keep * 0.25).astype(jnp.bfloat16)


def draw_degree_caps(key, part):
    rows_out, cols_out, mask_out = tile_layout(key)
    keep = tile_keep(key)
    row_count = jnp.sum(keep.astype(jnp.int32), axis=-1) * mask_out[..., None]
    dev_row = jnp.arange(N_ROW, dtype=jnp.int32)[:, None, None]
    global_block = dev_row * RBLK + rows_out
    node_ids = global_block[..., None] * BLK + jnp.arange(BLK, dtype=jnp.int32)[None, None, None, :]
    counts = jax.ops.segment_sum(row_count.reshape(-1), node_ids.reshape(-1), num_segments=NODES)
    return jnp.clip(counts, 1, 32).astype(jnp.int32)


def draw_features(key, part):
    key_col, key_value = jax.random.split(jax.random.fold_in(key, 13))
    col_scale = jnp.exp(jax.random.uniform(key_col, (HID,), jnp.float32) * math.log(10.0))
    values = jax.random.normal(key_value, (NODES, HID), jnp.float32)
    return (values * col_scale[None, :] * 0.4).astype(jnp.bfloat16)


def draw_out_grad(key, part):
    key_row, key_col, key_value = jax.random.split(jax.random.fold_in(key, 17), 3)
    row_scale = jnp.exp(jax.random.uniform(key_row, (NODES,), jnp.float32) * math.log(10.0))
    col_scale = jnp.exp(jax.random.uniform(key_col, (HID,), jnp.float32) * math.log(10.0))
    values = jax.random.normal(key_value, (NODES, HID), jnp.float32)
    return (values * row_scale[:, None] * col_scale[None, :] * 0.3).astype(jnp.bfloat16)


def touch_ends(values, key, smallest, top_value):
    longest = values.shape.index(max(values.shape))
    spots = []
    for shift in (0, 1):
        where = [jax.random.randint(jax.random.fold_in(key, axis), (), 0, length) for axis, length in enumerate(values.shape)]
        where[longest] = (where[longest] + shift) % values.shape[longest]
        spots.append(tuple(where))
    return values.at[spots[0]].set(smallest).at[spots[1]].set(top_value)


def shard_levels(key, shape, pieces, least, top_value):
    def one(dim, shards_of):
        draws = jax.random.uniform(jax.random.fold_in(jax.random.fold_in(key, 6), dim), (shards_of,), jnp.float32, least / len(pieces), top_value / len(pieces))
        return jnp.repeat(jnp.exp(draws), shape[dim] // shards_of).reshape((-1,) + (1,) * (len(shape) - dim - 1))

    level = one(*pieces[0])
    for cut in pieces[1:]:
        level = level * one(*cut)
    return level


def noise(stream_key, dims, deviation, bound, shards=(), kind=jnp.bfloat16):
    result = jax.random.normal(stream_key, dims, jnp.float32) * deviation
    if len(shards) > 0:
        result = shard_levels(stream_key, dims, shards, -0.22, 0.18) * result
    return jnp.clip(result, min=-bound, max=bound).astype(kind)


def setup_inputs(seed: int = 0) -> dict:
    key_of = jax.random.split(jax.random.key(seed), 12)
    return {
        "tile_values": draw_tile_values(jax.random.fold_in(key_of[11], 71), 0),
        "tile_rows": draw_tile_rows(jax.random.fold_in(key_of[11], 71), 0),
        "tile_cols": draw_tile_cols(jax.random.fold_in(key_of[11], 71), 0),
        "tile_mask": draw_tile_mask(jax.random.fold_in(key_of[11], 71), 0),
        "degree_caps": draw_degree_caps(jax.random.fold_in(key_of[11], 71), 0),
        "clip_groups": touch_ends(jax.random.randint(key_of[5], (NODES,), 0, GROUPS), jax.random.fold_in(key_of[5], 1), 0, GROUPS - 1).astype(jnp.int32),
        "clip_bounds": jnp.clip(jnp.exp(jax.random.uniform(key_of[6], (GROUPS,), jnp.float32, math.log(51.2), math.log(256.0))), 51.2, 256.0),
        "features": draw_features(jax.random.fold_in(key_of[11], 71), 0),
        "weight": noise(key_of[8], (HID, HID), HID ** -0.5, 0.375),
        "out_grad": draw_out_grad(jax.random.fold_in(key_of[11], 71), 0),
        "dp_noise": noise(key_of[10], (HID, HID), 1.0, 6.0, ((1, 2),), jnp.float32),
    }


def reference(tile_values, tile_rows, tile_cols, tile_mask, degree_caps, clip_groups, clip_bounds, features, weight, out_grad, dp_noise):
    row_span = NODE_DEV * N_COL
    col_span = NODE_DEV * N_ROW
    width = features.shape[1]
    feat_full = features.astype(jnp.float32)
    device_ids = jnp.arange(N_ROW * N_COL, dtype=jnp.int32)

    def forward_step(totals, device):
        row_idx = device // N_COL
        col_idx = device % N_COL
        tile_vals = tile_values[row_idx, col_idx].astype(jnp.float32)
        source = lax.dynamic_slice_in_dim(feat_full, (col_idx * col_span).astype(jnp.int32), col_span, 0)
        source = source.reshape(CBLK, BLK, width)
        picked = source[tile_cols[row_idx, col_idx]]
        products = jnp.einsum('kij,kjf->kif', tile_vals, picked)
        target = jnp.where(tile_mask[row_idx, col_idx] == 1, tile_rows[row_idx, col_idx], RBLK)
        part_sum = jax.ops.segment_sum(products, target, num_segments=RBLK + 1)[:RBLK].reshape(row_span, width)
        start = (row_idx * row_span).astype(jnp.int32)
        old_sum = lax.dynamic_slice_in_dim(totals, start, row_span, 0)
        return (lax.dynamic_update_slice_in_dim(totals, old_sum + part_sum, start, 0), None)
    raw_sum, _ = lax.scan(forward_step, jnp.zeros((NODES, width), jnp.float32), device_ids)
    node_scale = lax.rsqrt(degree_caps.astype(jnp.float32))[:, None]
    aggregate = (raw_sum * node_scale).astype(jnp.bfloat16)
    pre_act = jnp.dot(aggregate, weight, preferred_element_type=jnp.float32)
    out_feat = jax.nn.silu(pre_act).astype(jnp.bfloat16)
    gate_sig = jax.nn.sigmoid(pre_act)
    grad_pre = (out_grad.astype(jnp.float32) * gate_sig * (1.0 + pre_act * (1.0 - gate_sig))).astype(jnp.bfloat16)
    agg_sq = lax.optimization_barrier(jnp.sum(jnp.square(aggregate.astype(jnp.float32)), axis=1))
    grad_sq = lax.optimization_barrier(jnp.sum(jnp.square(grad_pre.astype(jnp.float32)), axis=1))
    bounds = clip_bounds[clip_groups]
    factor = jnp.minimum(1.0, bounds / (jnp.sqrt(agg_sq + 1e-06) * jnp.sqrt(grad_sq + 1e-06)))
    clipped = (factor[:, None] * grad_pre.astype(jnp.float32)).astype(jnp.bfloat16)
    total_grad = jnp.dot(aggregate.T, clipped, preferred_element_type=jnp.float32)
    grad_weight = total_grad * (1.0 / math.sqrt(NODES)) + dp_noise
    back_prod = jnp.dot(grad_pre, weight.T, preferred_element_type=jnp.float32)
    grad_agg = (back_prod * node_scale).astype(jnp.bfloat16)
    grad_full = grad_agg.astype(jnp.float32)

    def backward_step(totals, device):
        row_idx = device // N_COL
        col_idx = device % N_COL
        tile_vals = tile_values[row_idx, col_idx].astype(jnp.float32)
        source = lax.dynamic_slice_in_dim(grad_full, (row_idx * row_span).astype(jnp.int32), row_span, 0)
        source = source.reshape(RBLK, BLK, width)
        picked = source[tile_rows[row_idx, col_idx]]
        products = jnp.einsum('kji,kjf->kif', tile_vals, picked)
        target = jnp.where(tile_mask[row_idx, col_idx] == 1, tile_cols[row_idx, col_idx], CBLK)
        part_sum = jax.ops.segment_sum(products, target, num_segments=CBLK + 1)[:CBLK].reshape(col_span, width)
        start = (col_idx * col_span).astype(jnp.int32)
        old_sum = lax.dynamic_slice_in_dim(totals, start, col_span, 0)
        return (lax.dynamic_update_slice_in_dim(totals, old_sum + part_sum, start, 0), None)
    input_sum, _ = lax.scan(backward_step, jnp.zeros((NODES, width), jnp.float32), device_ids)
    grad_input = input_sum.astype(jnp.bfloat16)
    return (out_feat, grad_weight, grad_input)
```

```python
import functools
import math

import jax
import jax.numpy as jnp
from jax import lax
from jax.experimental import pallas as pl
from jax.experimental.pallas import tpu as pltpu
from jax.sharding import PartitionSpec as P

MESH = pl.DeviceIdType.MESH
PIECE = 256
LAG = 2


def layer(
    n_row, n_col, scale, cached,
    map_ref, bounds_ref, tiles_hbm, feats, weight, out_grad, noise, caps, groups,
    out_feat, grad_weight, grad_input,
    tiles, dense, rs_send, rs_recv, own, og_peer, agg, grads, acc,
    w_local, w_col, w_row, w_all, z_left, z_right, z_send, z_sum,
    tile_sem, og_sem, agg_sem, rs_ssem, rs_rsem, ag_ssem, ag_rsem,
    wc_ssem, wc_rsem, wr_ssem, wr_rsem, wa_ssem, wa_rsem,
    z_ssem, zl_rsem, zr_rsem, fin_ssem, fin_rsem,
):
    row, col, feat = lax.axis_index("row"), lax.axis_index("col"), lax.axis_index("feat")
    other = 1 - feat
    slots, blk = tiles_hbm.shape[0], tiles_hbm.shape[1]
    node, half = out_grad.shape
    col_blocks = feats.shape[0] // blk
    sub = node // blk
    w_rows = w_col.shape[1]
    pieces = z_send.shape[0]

    def remote(src, dst, ssem, rsem, where):
        return pltpu.make_async_remote_copy(
            src_ref=src, dst_ref=dst, send_sem=ssem, recv_sem=rsem,
            device_id=where, device_id_type=MESH,
        )

    load = pltpu.make_async_copy(tiles_hbm, tiles.at[pl.ds(0, slots)], tile_sem)
    load.start()

    barrier = pltpu.get_barrier_semaphore()
    pl.semaphore_signal(barrier, inc=1, device_id={"feat": other}, device_id_type=MESH)
    for step in range(1, n_col):
        pl.semaphore_signal(barrier, inc=1, device_id={"col": lax.rem(col + step, n_col)}, device_id_type=MESH)
    for step in range(1, n_row):
        pl.semaphore_signal(barrier, inc=1, device_id={"row": lax.rem(row + step, n_row)}, device_id_type=MESH)
    tiles[slots] = jnp.zeros((blk, blk), jnp.bfloat16)
    pl.semaphore_wait(barrier, n_col + n_row - 1)

    og_copy = remote(out_grad, og_peer, og_sem.at[0], og_sem.at[1], {"feat": other})
    og_copy.start()
    load.wait()

    def assemble(chunk, slot):
        for rb in range(sub):
            for cb in range(col_blocks):
                which = map_ref[(chunk * sub + rb) * col_blocks + cb]
                dense[slot, rb * blk:(rb + 1) * blk, cb * blk:(cb + 1) * blk] = tiles[which]

    def rs_copy(dest, sender):
        return remote(rs_send.at[dest], rs_recv.at[sender], rs_ssem.at[dest], rs_rsem.at[sender], {"col": dest})

    def forward(step, carry):
        chunk = lax.rem(col + 1 + step, n_col)
        slot = chunk if cached else 0
        assemble(chunk, slot)
        part = jnp.dot(dense[slot], feats[...], preferred_element_type=jnp.float32)

        @pl.when(step < n_col - 1)
        def _():
            rs_send[chunk] = part.astype(jnp.bfloat16)
            rs_copy(chunk, col).start()

        @pl.when(step == n_col - 1)
        def _():
            own[...] = part

        return carry

    lax.fori_loop(0, n_col, forward, 0)

    node_scale = jnp.transpose(jnp.broadcast_to(lax.rsqrt(caps[...].astype(jnp.float32)), (half, node)))
    bound = jnp.zeros((1, node), jnp.float32)
    for g in range(bounds_ref.shape[0]):
        bound = bound + jnp.where(groups[...] == g, bounds_ref[g], 0.0)
    bound = jnp.transpose(jnp.broadcast_to(bound, (half, node)))

    for step in range(1, n_col):
        peer = lax.rem(col - step + n_col, n_col)
        rs_copy(peer, peer).wait_recv()
        own[...] += rs_recv[peer].astype(jnp.float32)
    agg[feat] = (own[...] * node_scale).astype(jnp.bfloat16)
    agg_copy = remote(agg.at[feat], agg.at[feat], agg_sem.at[0], agg_sem.at[1], {"feat": other})
    agg_copy.start()
    og_copy.wait()
    agg_copy.wait()

    mine = pl.ds(pl.multiple_of(feat * half, half), half)
    theirs = pl.ds(pl.multiple_of(other * half, half), half)
    agg_0, agg_1 = agg[0], agg[1]

    def activation(columns):
        return jnp.dot(agg_0, weight[:half, columns], preferred_element_type=jnp.float32) + jnp.dot(
            agg_1, weight[half:, columns], preferred_element_type=jnp.float32
        )

    def gated(pre, cotangent):
        sig = 1.0 / (1.0 + jnp.exp(-pre))
        return sig, (cotangent.astype(jnp.float32) * sig * (1.0 + pre * (1.0 - sig))).astype(jnp.bfloat16)

    pre_mine = activation(mine)
    sig_mine, grad_mine = gated(pre_mine, out_grad[...])
    _, grad_theirs = gated(activation(theirs), og_peer[...])
    dims = (((1,), (1,)), ((), ()))
    back = lax.dot_general(grad_mine, weight[mine, mine], dims, preferred_element_type=jnp.float32)
    back += lax.dot_general(grad_theirs, weight[mine, theirs], dims, preferred_element_type=jnp.float32)
    grads[col] = jnp.transpose(back * node_scale).astype(jnp.bfloat16)

    def ag_copy(peer, sender):
        return remote(grads.at[sender], grads.at[sender], ag_ssem.at[peer], ag_rsem.at[sender], {"col": peer})

    for step in range(1, n_col):
        ag_copy(lax.rem(col + step, n_col), col).start()

    out_feat[...] = (pre_mine * sig_mine).astype(jnp.bfloat16)

    def squares(a, b):
        a, b = a.astype(jnp.float32), b.astype(jnp.float32)
        return jnp.sum(a * a + b * b, axis=1, keepdims=True)

    norm = jnp.sqrt(squares(agg_0, agg_1) + 1e-06) * jnp.sqrt(squares(grad_mine, grad_theirs) + 1e-06)
    factor = jnp.minimum(1.0, bound / norm)
    clipped = (factor * grad_mine.astype(jnp.float32)).astype(jnp.bfloat16)
    dims = (((0,), (0,)), ((), ()))
    w_local[:half] = lax.dot_general(agg_0, clipped, dims, preferred_element_type=jnp.float32)
    w_local[half:] = lax.dot_general(agg_1, clipped, dims, preferred_element_type=jnp.float32)

    def w_part(index):
        return w_local.at[pl.ds(pl.multiple_of(index * w_rows, w_rows), w_rows)]

    def wc_copy(dest, sender):
        return remote(w_part(dest), w_col.at[sender], wc_ssem.at[dest], wc_rsem.at[sender], {"col": dest})

    def wr_copy(dest, sender):
        return remote(w_row.at[sender], w_row.at[sender], wr_ssem.at[dest], wr_rsem.at[sender], {"row": dest})

    def wa_copy(dest, sender):
        return remote(w_all.at[sender], w_all.at[sender], wa_ssem.at[dest], wa_rsem.at[sender], {"col": dest})

    for step in range(1, n_col):
        wc_copy(lax.rem(col + step, n_col), col).start()

    def backward(peer):
        slot = peer if cached else 0
        if not cached:
            assemble(peer, slot)
        return jnp.dot(grads[peer], dense[slot], preferred_element_type=jnp.float32)

    acc[...] = backward(col)

    total = w_part(col)[...]
    for step in range(1, n_col):
        peer = lax.rem(col - step + n_col, n_col)
        wc_copy(peer, peer).wait_recv()
        total += w_col[peer]
    w_row[row] = total
    for step in range(1, n_row):
        wr_copy(lax.rem(row + step, n_row), row).start()

    def backward_step(step, carry):
        peer = lax.rem(col - step + n_col, n_col)
        ag_copy(peer, peer).wait_recv()
        acc[...] += backward(peer)
        return carry

    lax.fori_loop(1, n_col, backward_step, 0)

    def fold_rows():
        for step in range(1, n_row):
            peer = lax.rem(row - step + n_row, n_row)
            wr_copy(peer, peer).wait_recv()
        total = w_row[0]
        for index in range(1, n_row):
            total += w_row[index]
        w_all[col] = total
        for step in range(1, n_col):
            wa_copy(lax.rem(col + step, n_col), col).start()

    def middle(p):
        return n_row // 2 - 1 if p % 2 == 0 else n_row // 2

    def z_up(p):
        return remote(z_send.at[p], z_left.at[p], z_ssem.at[p], zl_rsem.at[p], {"row": row + 1})

    def z_down(p):
        return remote(z_send.at[p], z_right.at[p], z_ssem.at[p], zr_rsem.at[p], {"row": row - 1})

    def final(p, way):
        spot = grad_input.at[pl.ds(p * PIECE, PIECE)]
        return remote(spot, spot, fin_ssem.at[way, p], fin_rsem.at[p], {"row": row + 1 if way else row - 1})

    last = n_row - 1

    def reduce_piece(p):
        mid = middle(p)
        z_sum[...] = jnp.transpose(acc[:, p * PIECE:(p + 1) * PIECE])

        @pl.when((row <= mid) & (row > 0))
        def _():
            z_up(p).wait_recv()
            z_sum[...] += z_left[p].astype(jnp.float32)

        @pl.when((row >= mid) & (row < last))
        def _():
            z_down(p).wait_recv()
            z_sum[...] += z_right[p].astype(jnp.float32)

        @pl.when(row < mid)
        def _():
            z_send[p] = z_sum[...].astype(jnp.bfloat16)
            z_up(p).start()

        @pl.when(row > mid)
        def _():
            z_send[p] = z_sum[...].astype(jnp.bfloat16)
            z_down(p).start()

        @pl.when(row == mid)
        def _():
            grad_input[p * PIECE:(p + 1) * PIECE] = z_sum[...].astype(jnp.bfloat16)

        @pl.when((row == mid) & (row > 0))
        def _():
            final(p, 0).start()

        @pl.when((row == mid) & (row < last))
        def _():
            final(p, 1).start()

    def finish_piece(p):
        mid = middle(p)

        @pl.when(row != mid)
        def _():
            final(p, 0).wait_recv()

        @pl.when((row < mid) & (row > 0))
        def _():
            final(p, 0).start()

        @pl.when((row > mid) & (row < last))
        def _():
            final(p, 1).start()

    for p in range(pieces + LAG):
        if p < pieces:
            reduce_piece(p)
        if p == 1:
            fold_rows()
        if p >= LAG:
            finish_piece(p - LAG)

    for step in range(1, n_col):
        peer = lax.rem(col - step + n_col, n_col)
        wa_copy(peer, peer).wait_recv()
    for index in range(n_col):
        spot = pl.ds(index * w_rows, w_rows)
        grad_weight[spot] = w_all[index] * scale + noise[spot]

    for step in range(1, n_col):
        peer = lax.rem(col + step, n_col)
        rs_copy(peer, col).wait_send()
        ag_copy(peer, col).wait_send()
        wc_copy(peer, col).wait_send()
        wa_copy(peer, col).wait_send()
    for step in range(1, n_row):
        wr_copy(lax.rem(row + step, n_row), row).wait_send()
    for p in range(pieces):
        mid = middle(p)

        @pl.when(row < mid)
        def _():
            z_up(p).wait_send()

        @pl.when(row > mid)
        def _():
            z_down(p).wait_send()

        @pl.when((row <= mid) & (row > 0))
        def _():
            final(p, 0).wait_send()

        @pl.when((row >= mid) & (row < last))
        def _():
            final(p, 1).wait_send()


def per_device(
    tile_values, tile_rows, tile_cols, tile_mask, degree_caps, clip_groups,
    clip_bounds, features, weight, out_grad, dp_noise,
):
    tile_vals = tile_values[0, 0]
    slots, blk = tile_vals.shape[0], tile_vals.shape[1]
    node, half = out_grad.shape
    n_col, n_row = lax.axis_size("col"), lax.axis_size("row")
    col_range = features.shape[0]
    row_blocks, col_blocks = node * n_col // blk, col_range // blk
    hid = weight.shape[0]
    pair = jnp.where(tile_mask[0, 0] == 1, tile_rows[0, 0] * col_blocks + tile_cols[0, 0], -1)
    wanted = jnp.arange(row_blocks * col_blocks, dtype=jnp.int32)
    order = jnp.arange(slots, dtype=jnp.int32)
    slot_map = jnp.min(jnp.where(pair[:, None] == wanted[None, :], order[:, None], slots), axis=0)
    cached = row_blocks * col_blocks * blk * blk * 2 <= (20 << 20)
    pieces = col_range // PIECE
    bf16, f32 = jnp.bfloat16, jnp.float32
    vmem, smem = pl.BlockSpec(memory_space=pltpu.VMEM), pl.BlockSpec(memory_space=pltpu.SMEM)
    sem = pltpu.SemaphoreType.DMA
    call = pl.pallas_call(
        functools.partial(layer, n_row, n_col, 1.0 / math.sqrt(node * n_col * n_row), cached),
        out_shape=(
            jax.ShapeDtypeStruct((node, half), bf16),
            jax.ShapeDtypeStruct((hid, half), f32),
            jax.ShapeDtypeStruct((col_range, half), bf16),
        ),
        in_specs=[smem, smem, pl.BlockSpec(memory_space=pl.ANY)] + [vmem] * 6,
        out_specs=(vmem, vmem, vmem),
        scratch_shapes=[
            pltpu.VMEM((slots + 1, blk, blk), bf16),
            pltpu.VMEM((n_col if cached else 1, node, col_range), bf16),
            pltpu.VMEM((n_col, node, half), bf16),
            pltpu.VMEM((n_col, node, half), bf16),
            pltpu.VMEM((node, half), f32),
            pltpu.VMEM((node, half), bf16),
            pltpu.VMEM((2, node, half), bf16),
            pltpu.VMEM((n_col, half, node), bf16),
            pltpu.VMEM((half, col_range), f32),
            pltpu.VMEM((hid, half), f32),
            pltpu.VMEM((n_col, hid // n_col, half), f32),
            pltpu.VMEM((n_row, hid // n_col, half), f32),
            pltpu.VMEM((n_col, hid // n_col, half), f32),
            pltpu.VMEM((pieces, PIECE, half), bf16),
            pltpu.VMEM((pieces, PIECE, half), bf16),
            pltpu.VMEM((pieces, PIECE, half), bf16),
            pltpu.VMEM((PIECE, half), f32),
            sem, sem((2,)), sem((2,)),
            sem((n_col,)), sem((n_col,)), sem((n_col,)), sem((n_col,)),
            sem((n_col,)), sem((n_col,)), sem((n_row,)), sem((n_row,)),
            sem((n_col,)), sem((n_col,)),
            sem((pieces,)), sem((pieces,)), sem((pieces,)), sem((2, pieces)), sem((pieces,)),
        ],
        compiler_params=pltpu.CompilerParams(
            collective_id=0, has_side_effects=True, vmem_limit_bytes=56 << 20
        ),
        name="layer",
    )
    return call(
        slot_map, clip_bounds, tile_vals, features, weight, out_grad, dp_noise,
        degree_caps[None, :], clip_groups[None, :],
    )


def solution(mesh):
    placed = (
        P("row", "col", None, None, None),
        P("row", "col", None),
        P("row", "col", None),
        P("row", "col", None),
        P(("row", "col")),
        P(("row", "col")),
        P(),
        P("col", "feat"),
        P(),
        P(("row", "col"), "feat"),
        P(None, "feat"),
    )
    return jax.shard_map(
        per_device,
        mesh=mesh,
        in_specs=placed,
        out_specs=(P(("row", "col"), "feat"), P(None, "feat"), P("col", "feat")),
        check_vma=False,
    )
```

```python
import functools
import math

import jax
import jax.numpy as jnp
from jax import lax
from jax.experimental import pallas as pl
from jax.experimental.pallas import tpu as pltpu
from jax.sharding import PartitionSpec as P

MESH = pl.DeviceIdType.MESH
PIECE = 256
LEAD = 1
LAG = 1
LOADS = 4


def layer(
    n_row, n_col, scale, cached,
    map_ref, bounds_ref, tiles_hbm, feats_hbm, weight_hbm, og_hbm, noise_hbm, caps, groups,
    out_feat_hbm, grad_weight_hbm, grad_input_hbm,
    feats, weight, out_grad, noise, out_feat, grad_weight, grad_input,
    tiles, dense, rs_send, rs_recv, own, og_peer, agg, grads, acc,
    w_local, w_col, w_row, w_all, z_left, z_right, z_send, z_sum,
    tile_sem, in_sem, out_sem, gin_sem, og_sem, agg_sem, rs_ssem, rs_rsem, ag_ssem, ag_rsem,
    wc_ssem, wc_rsem, wr_ssem, wr_rsem, wa_ssem, wa_rsem,
    z_ssem, zl_rsem, zr_rsem, fin_ssem, fin_rsem,
):
    row, col, feat = lax.axis_index("row"), lax.axis_index("col"), lax.axis_index("feat")
    other = 1 - feat
    slots, blk = tiles_hbm.shape[0], tiles_hbm.shape[1]
    node, half = og_hbm.shape
    col_blocks = feats.shape[0] // blk
    sub = node // blk
    w_rows = w_col.shape[1]
    pieces = z_send.shape[0]

    def remote(src, dst, ssem, rsem, where):
        return pltpu.make_async_remote_copy(
            src_ref=src, dst_ref=dst, send_sem=ssem, recv_sem=rsem,
            device_id=where, device_id_type=MESH,
        )

    count = slots // LOADS
    loads = [
        pltpu.make_async_copy(
            tiles_hbm.at[pl.ds(i * count, count)], tiles.at[pl.ds(i * count, count)], tile_sem.at[i]
        )
        for i in range(LOADS)
    ]
    inputs = [
        pltpu.make_async_copy(src, dst, in_sem.at[i])
        for i, (src, dst) in enumerate(
            ((feats_hbm, feats), (og_hbm, out_grad), (weight_hbm, weight), (noise_hbm, noise))
        )
    ]
    for copy in loads + inputs:
        copy.start()

    barrier = pltpu.get_barrier_semaphore()
    pl.semaphore_signal(barrier, inc=1, device_id={"feat": other}, device_id_type=MESH)
    for step in range(1, n_col):
        pl.semaphore_signal(barrier, inc=1, device_id={"col": lax.rem(col + step, n_col)}, device_id_type=MESH)
    for step in range(1, n_row):
        pl.semaphore_signal(barrier, inc=1, device_id={"row": lax.rem(row + step, n_row)}, device_id_type=MESH)
    tiles[slots] = jnp.zeros((blk, blk), jnp.bfloat16)
    pl.semaphore_wait(barrier, n_col + n_row - 1)

    og_copy = remote(og_hbm, og_peer, og_sem.at[0], og_sem.at[1], {"feat": other})
    og_copy.start()
    for copy in loads + inputs:
        copy.wait()

    def assemble(chunk, slot):
        for rb in range(sub):
            for cb in range(col_blocks):
                which = map_ref[(chunk * sub + rb) * col_blocks + cb]
                dense[slot, rb * blk:(rb + 1) * blk, cb * blk:(cb + 1) * blk] = tiles[which]

    def rs_copy(dest, sender):
        return remote(rs_send.at[dest], rs_recv.at[sender], rs_ssem.at[dest], rs_rsem.at[sender], {"col": dest})

    def forward(step, carry):
        chunk = lax.rem(col + 1 + step, n_col)
        slot = chunk if cached else 0
        assemble(chunk, slot)
        part = jnp.dot(dense[slot], feats[...], preferred_element_type=jnp.float32)

        @pl.when(step < n_col - 1)
        def _():
            rs_send[chunk] = part.astype(jnp.bfloat16)
            rs_copy(chunk, col).start()

        @pl.when(step == n_col - 1)
        def _():
            own[...] = part

        return carry

    lax.fori_loop(0, n_col, forward, 0)

    node_scale = jnp.transpose(jnp.broadcast_to(lax.rsqrt(caps[...].astype(jnp.float32)), (half, node)))
    bound = jnp.zeros((1, node), jnp.float32)
    for g in range(bounds_ref.shape[0]):
        bound = bound + jnp.where(groups[...] == g, bounds_ref[g], 0.0)
    bound = jnp.transpose(jnp.broadcast_to(bound, (half, node)))

    for step in range(1, n_col):
        peer = lax.rem(col - step + n_col, n_col)
        rs_copy(peer, peer).wait_recv()
        own[...] += rs_recv[peer].astype(jnp.float32)
    agg[feat] = (own[...] * node_scale).astype(jnp.bfloat16)
    agg_copy = remote(agg.at[feat], agg.at[feat], agg_sem.at[0], agg_sem.at[1], {"feat": other})
    agg_copy.start()
    og_copy.wait()
    agg_copy.wait()

    mine = pl.ds(pl.multiple_of(feat * half, half), half)
    theirs = pl.ds(pl.multiple_of(other * half, half), half)
    agg_0, agg_1 = agg[0], agg[1]

    def activation(columns):
        return jnp.dot(agg_0, weight[:half, columns], preferred_element_type=jnp.float32) + jnp.dot(
            agg_1, weight[half:, columns], preferred_element_type=jnp.float32
        )

    def gated(pre, cotangent):
        sig = 1.0 / (1.0 + jnp.exp(-pre))
        return sig, (cotangent.astype(jnp.float32) * sig * (1.0 + pre * (1.0 - sig))).astype(jnp.bfloat16)

    pre_mine = activation(mine)
    sig_mine, grad_mine = gated(pre_mine, out_grad[...])
    _, grad_theirs = gated(activation(theirs), og_peer[...])
    dims = (((1,), (1,)), ((), ()))
    back = lax.dot_general(grad_mine, weight[mine, mine], dims, preferred_element_type=jnp.float32)
    back += lax.dot_general(grad_theirs, weight[mine, theirs], dims, preferred_element_type=jnp.float32)
    grads[col] = jnp.transpose(back * node_scale).astype(jnp.bfloat16)

    def ag_copy(peer, sender):
        return remote(grads.at[sender], grads.at[sender], ag_ssem.at[peer], ag_rsem.at[sender], {"col": peer})

    for step in range(1, n_col):
        ag_copy(lax.rem(col + step, n_col), col).start()

    out_feat[...] = (pre_mine * sig_mine).astype(jnp.bfloat16)
    feat_out = pltpu.make_async_copy(out_feat, out_feat_hbm, out_sem.at[0])
    feat_out.start()

    def squares(a, b):
        a, b = a.astype(jnp.float32), b.astype(jnp.float32)
        return jnp.sum(a * a + b * b, axis=1, keepdims=True)

    norm = jnp.sqrt(squares(agg_0, agg_1) + 1e-06) * jnp.sqrt(squares(grad_mine, grad_theirs) + 1e-06)
    factor = jnp.minimum(1.0, bound / norm)
    clipped = (factor * grad_mine.astype(jnp.float32)).astype(jnp.bfloat16)
    dims = (((0,), (0,)), ((), ()))
    w_local[:half] = lax.dot_general(agg_0, clipped, dims, preferred_element_type=jnp.float32)
    w_local[half:] = lax.dot_general(agg_1, clipped, dims, preferred_element_type=jnp.float32)

    def w_part(index):
        return w_local.at[pl.ds(pl.multiple_of(index * w_rows, w_rows), w_rows)]

    def wc_copy(dest, sender):
        return remote(w_part(dest), w_col.at[sender], wc_ssem.at[dest], wc_rsem.at[sender], {"col": dest})

    def wr_copy(dest, sender):
        return remote(w_row.at[sender], w_row.at[sender], wr_ssem.at[dest], wr_rsem.at[sender], {"row": dest})

    def wa_copy(dest, sender):
        return remote(w_all.at[sender], w_all.at[sender], wa_ssem.at[dest], wa_rsem.at[sender], {"col": dest})

    for step in range(1, n_col):
        wc_copy(lax.rem(col + step, n_col), col).start()

    def backward(peer):
        slot = peer if cached else 0
        if not cached:
            assemble(peer, slot)
        return jnp.dot(grads[peer], dense[slot], preferred_element_type=jnp.float32)

    acc[...] = backward(col)

    total = w_part(col)[...]
    for step in range(1, n_col):
        peer = lax.rem(col - step + n_col, n_col)
        wc_copy(peer, peer).wait_recv()
        total += w_col[peer]
    w_row[row] = total
    for step in range(1, n_row):
        wr_copy(lax.rem(row + step, n_row), row).start()

    def backward_step(step, carry):
        peer = lax.rem(col - step + n_col, n_col)
        ag_copy(peer, peer).wait_recv()
        acc[...] += backward(peer)
        return carry

    lax.fori_loop(1, n_col - 1, backward_step, 0)

    tail = lax.rem(col + 1, n_col)
    tail_slot = tail if cached else 0
    if not cached:
        assemble(tail, tail_slot)
    ag_copy(tail, tail).wait_recv()

    def fold_rows():
        for step in range(1, n_row):
            peer = lax.rem(row - step + n_row, n_row)
            wr_copy(peer, peer).wait_recv()
        total = w_row[0]
        for index in range(1, n_row):
            total += w_row[index]
        w_all[col] = total
        for step in range(1, n_col):
            wa_copy(lax.rem(col + step, n_col), col).start()

    last = n_row - 1
    pairs = pieces // 2
    lower = row < n_row // 2
    odd = jnp.where(lower, 1, 0)
    mid = jnp.where(lower, n_row // 2 - 1, n_row // 2)
    is_mid = row == mid

    def span(p):
        return pl.ds(pl.multiple_of(p * PIECE, PIECE), PIECE)

    def send_up(p):
        return remote(z_send.at[p], z_left.at[p], z_ssem.at[p], zl_rsem.at[p], {"row": row + 1})

    def send_down(p):
        return remote(z_send.at[p], z_right.at[p], z_ssem.at[p], zr_rsem.at[p], {"row": row - 1})

    def final(p, way):
        spot = grad_input.at[p]
        return remote(spot, spot, fin_ssem.at[way, p], fin_rsem.at[p], {"row": row + 1 if way else row - 1})

    def store(p):
        return pltpu.make_async_copy(grad_input.at[p], grad_input_hbm.at[span(p)], gin_sem.at[p])

    def own_part(p):
        product = jnp.dot(grads[tail], dense[tail_slot, :, span(p)], preferred_element_type=jnp.float32)
        z_sum[...] = jnp.transpose(acc[:, span(p)] + product)

    def add_left(p, when):
        @pl.when(when)
        def _():
            send_up(p).wait_recv()
            z_sum[...] += z_left[p].astype(jnp.float32)

    def add_right(p, when):
        @pl.when(when)
        def _():
            send_down(p).wait_recv()
            z_sum[...] += z_right[p].astype(jnp.float32)

    def pass_on(p, up, down):
        @pl.when(up | down)
        def _():
            z_send[p] = z_sum[...].astype(jnp.bfloat16)

        @pl.when(up)
        def _():
            send_up(p).start()

        @pl.when(down)
        def _():
            send_down(p).start()

    def first_piece(j):
        p = 2 * j + odd
        own_part(p)
        add_left(p, lower & (row > 0))
        add_right(p, (row >= n_row // 2) & (row < last))
        pass_on(p, lower, row >= n_row // 2)

    def second_piece(j):
        p = 2 * j + 1 - odd
        own_part(p)
        add_left(p, (row > 0) & (row <= n_row // 2))
        add_right(p, (row < last) & (row >= n_row // 2 - 1))
        pass_on(p, row < n_row // 2 - 1, row > n_row // 2)

        @pl.when(is_mid)
        def _():
            grad_input[p] = z_sum[...].astype(jnp.bfloat16)

        @pl.when(is_mid & (row < last))
        def _():
            final(p, 1).start()

        @pl.when(is_mid & (row > 0))
        def _():
            final(p, 0).start()

    def finish(p, wait):
        @pl.when(wait)
        def _():
            final(p, 0).wait_recv()

        @pl.when(wait & lower & (row > 0))
        def _():
            final(p, 0).start()

        @pl.when(wait & (row >= n_row // 2) & (row < last))
        def _():
            final(p, 1).start()

        store(p).start()

    def z_step(j, carry):
        @pl.when(j < pairs)
        def _():
            first_piece(j)

        @pl.when((j >= LEAD) & (j < pairs + LEAD))
        def _():
            second_piece(j - LEAD)

        @pl.when(j >= LEAD + LAG)
        def _():
            done = j - LEAD - LAG
            finish(2 * done + odd, row >= 0)
            finish(2 * done + 1 - odd, row != mid)

        return carry

    lax.fori_loop(0, 1, z_step, 0)
    fold_rows()
    lax.fori_loop(1, pairs + LEAD + LAG, z_step, 0)

    for step in range(1, n_col):
        peer = lax.rem(col - step + n_col, n_col)
        wa_copy(peer, peer).wait_recv()
    for index in range(n_col):
        spot = pl.ds(index * w_rows, w_rows)
        grad_weight[spot] = w_all[index] * scale + noise[spot]
    weight_out = pltpu.make_async_copy(grad_weight, grad_weight_hbm, out_sem.at[1])
    weight_out.start()

    for step in range(1, n_col):
        peer = lax.rem(col + step, n_col)
        rs_copy(peer, col).wait_send()
        ag_copy(peer, col).wait_send()
        wc_copy(peer, col).wait_send()
        wa_copy(peer, col).wait_send()
    for step in range(1, n_row):
        wr_copy(lax.rem(row + step, n_row), row).wait_send()

    def drain(j, carry):
        for p, passed, done in (
            (2 * j + odd, row >= 0, row < 0),
            (2 * j + 1 - odd, row != mid, is_mid),
        ):
            @pl.when(passed)
            def _():
                send_up(p).wait_send()

            @pl.when((lower | done) & (row > 0))
            def _():
                final(p, 0).wait_send()

            @pl.when(((row >= n_row // 2) | done) & (row < last))
            def _():
                final(p, 1).wait_send()

            store(p).wait()
        return carry

    lax.fori_loop(0, pairs, drain, 0)
    feat_out.wait()
    weight_out.wait()


def deliver(a_in, b_in, c_in, a_out, b_out, c_out, sems):
    copies = [
        pltpu.make_async_copy(src, dst, sems.at[i])
        for i, (src, dst) in enumerate(((a_in, a_out), (b_in, b_out), (c_in, c_out)))
    ]
    for copy in copies:
        copy.start()
    for copy in copies:
        copy.wait()


def per_device(
    tile_values, tile_rows, tile_cols, tile_mask, degree_caps, clip_groups,
    clip_bounds, features, weight, out_grad, dp_noise,
):
    tile_vals = tile_values[0, 0]
    slots, blk = tile_vals.shape[0], tile_vals.shape[1]
    node, half = out_grad.shape
    n_col, n_row = lax.axis_size("col"), lax.axis_size("row")
    col_range = features.shape[0]
    row_blocks, col_blocks = node * n_col // blk, col_range // blk
    hid = weight.shape[0]
    pair = jnp.where(tile_mask[0, 0] == 1, tile_rows[0, 0] * col_blocks + tile_cols[0, 0], -1)
    wanted = jnp.arange(row_blocks * col_blocks, dtype=jnp.int32)
    order = jnp.arange(slots, dtype=jnp.int32)
    slot_map = jnp.min(jnp.where(pair[:, None] == wanted[None, :], order[:, None], slots), axis=0)
    cached = row_blocks * col_blocks * blk * blk * 2 <= (20 << 20)
    pieces = col_range // PIECE
    bf16, f32 = jnp.bfloat16, jnp.float32
    vmem, smem = pl.BlockSpec(memory_space=pltpu.VMEM), pl.BlockSpec(memory_space=pltpu.SMEM)
    anywhere = pl.BlockSpec(memory_space=pl.ANY)
    sem = pltpu.SemaphoreType.DMA
    shapes = (
        jax.ShapeDtypeStruct((node, half), bf16),
        jax.ShapeDtypeStruct((hid, half), f32),
        jax.ShapeDtypeStruct((col_range, half), bf16),
    )
    call = pl.pallas_call(
        functools.partial(layer, n_row, n_col, 1.0 / math.sqrt(node * n_col * n_row), cached),
        out_shape=shapes,
        in_specs=[smem, smem] + [anywhere] * 5 + [vmem] * 2,
        out_specs=[anywhere] * 3,
        scratch_shapes=[
            pltpu.VMEM((col_range, half), bf16),
            pltpu.VMEM((hid, hid), bf16),
            pltpu.VMEM((node, half), bf16),
            pltpu.VMEM((hid, half), f32),
            pltpu.VMEM((node, half), bf16),
            pltpu.VMEM((hid, half), f32),
            pltpu.VMEM((pieces, PIECE, half), bf16),
            pltpu.VMEM((slots + 1, blk, blk), bf16),
            pltpu.VMEM((n_col if cached else 1, node, col_range), bf16),
            pltpu.VMEM((n_col, node, half), bf16),
            pltpu.VMEM((n_col, node, half), bf16),
            pltpu.VMEM((node, half), f32),
            pltpu.VMEM((node, half), bf16),
            pltpu.VMEM((2, node, half), bf16),
            pltpu.VMEM((n_col, half, node), bf16),
            pltpu.VMEM((half, col_range), f32),
            pltpu.VMEM((hid, half), f32),
            pltpu.VMEM((n_col, hid // n_col, half), f32),
            pltpu.VMEM((n_row, hid // n_col, half), f32),
            pltpu.VMEM((n_col, hid // n_col, half), f32),
            pltpu.VMEM((pieces, PIECE, half), bf16),
            pltpu.VMEM((pieces, PIECE, half), bf16),
            pltpu.VMEM((pieces, PIECE, half), bf16),
            pltpu.VMEM((PIECE, half), f32),
            sem((LOADS,)), sem((4,)), sem((2,)), sem((pieces,)), sem((2,)), sem((2,)),
            sem((n_col,)), sem((n_col,)), sem((n_col,)), sem((n_col,)),
            sem((n_col,)), sem((n_col,)), sem((n_row,)), sem((n_row,)),
            sem((n_col,)), sem((n_col,)),
            sem((pieces,)), sem((pieces,)), sem((pieces,)), sem((2, pieces)), sem((pieces,)),
        ],
        compiler_params=pltpu.CompilerParams(
            collective_id=0, has_side_effects=True, vmem_limit_bytes=56 << 20
        ),
        name="layer",
    )
    results = call(
        slot_map, clip_bounds, tile_vals, features, weight, out_grad, dp_noise,
        degree_caps[None, :], clip_groups[None, :],
    )
    return pl.pallas_call(
        deliver,
        out_shape=shapes,
        in_specs=[anywhere] * 3,
        out_specs=[anywhere] * 3,
        scratch_shapes=[sem((3,))],
        name="deliver",
    )(*results)


def solution(mesh):
    placed = (
        P("row", "col", None, None, None),
        P("row", "col", None),
        P("row", "col", None),
        P("row", "col", None),
        P(("row", "col")),
        P(("row", "col")),
        P(),
        P("col", "feat"),
        P(),
        P(("row", "col"), "feat"),
        P(None, "feat"),
    )
    return jax.shard_map(
        per_device,
        mesh=mesh,
        in_specs=placed,
        out_specs=(P(("row", "col"), "feat"), P(None, "feat"), P("col", "feat")),
        check_vma=False,
    )
```

```python
import functools
import math

import jax
import jax.numpy as jnp
from jax import lax
from jax.experimental import pallas as pl
from jax.experimental.pallas import tpu as pltpu
from jax.sharding import PartitionSpec as P

MESH = pl.DeviceIdType.MESH
PIECE = 256
LEAD = 2
LAG = 3
LOADS = 4


def layer(
    n_row, n_col, scale, cached,
    map_ref, bounds_ref, tiles_hbm, feats_hbm, weight_hbm, og_hbm, noise_hbm, caps, groups,
    out_feat_hbm, grad_weight_hbm, grad_input_hbm,
    feats, weight, out_grad, noise, out_feat, grad_weight, grad_input,
    tiles, dense, rs_send, rs_recv, own, og_peer, agg, grads, acc,
    w_local, w_col, w_row, w_all, z_left, z_right, z_send, z_sum,
    tile_sem, in_sem, out_sem, gin_sem, og_sem, agg_sem, rs_ssem, rs_rsem, ag_ssem, ag_rsem,
    wc_ssem, wc_rsem, wr_ssem, wr_rsem, wa_ssem, wa_rsem,
    z_ssem, zl_rsem, zr_rsem, fin_ssem, fin_rsem,
):
    row, col, feat = lax.axis_index("row"), lax.axis_index("col"), lax.axis_index("feat")
    other = 1 - feat
    slots, blk = tiles_hbm.shape[0], tiles_hbm.shape[1]
    node, half = og_hbm.shape
    col_blocks = feats.shape[0] // blk
    sub = node // blk
    w_rows = w_col.shape[1]
    pieces = z_send.shape[0]

    def remote(src, dst, ssem, rsem, where):
        return pltpu.make_async_remote_copy(
            src_ref=src, dst_ref=dst, send_sem=ssem, recv_sem=rsem,
            device_id=where, device_id_type=MESH,
        )

    count = slots // LOADS
    loads = [
        pltpu.make_async_copy(
            tiles_hbm.at[pl.ds(i * count, count)], tiles.at[pl.ds(i * count, count)], tile_sem.at[i]
        )
        for i in range(LOADS)
    ]
    inputs = [
        pltpu.make_async_copy(src, dst, in_sem.at[i])
        for i, (src, dst) in enumerate(
            ((feats_hbm, feats), (og_hbm, out_grad), (weight_hbm, weight), (noise_hbm, noise))
        )
    ]
    for copy in loads + inputs:
        copy.start()

    barrier = pltpu.get_barrier_semaphore()
    pl.semaphore_signal(barrier, inc=1, device_id={"feat": other}, device_id_type=MESH)
    for step in range(1, n_col):
        pl.semaphore_signal(barrier, inc=1, device_id={"col": lax.rem(col + step, n_col)}, device_id_type=MESH)
    for step in range(1, n_row):
        pl.semaphore_signal(barrier, inc=1, device_id={"row": lax.rem(row + step, n_row)}, device_id_type=MESH)
    tiles[slots] = jnp.zeros((blk, blk), jnp.bfloat16)
    pl.semaphore_wait(barrier, n_col + n_row - 1)

    og_copy = remote(og_hbm, og_peer, og_sem.at[0], og_sem.at[1], {"feat": other})
    og_copy.start()
    for copy in loads + inputs:
        copy.wait()

    def assemble(chunk, slot):
        for rb in range(sub):
            for cb in range(col_blocks):
                which = map_ref[(chunk * sub + rb) * col_blocks + cb]
                dense[slot, rb * blk:(rb + 1) * blk, cb * blk:(cb + 1) * blk] = tiles[which]

    def rs_copy(dest, sender):
        return remote(rs_send.at[dest], rs_recv.at[sender], rs_ssem.at[dest], rs_rsem.at[sender], {"col": dest})

    def forward(step, carry):
        chunk = lax.rem(col + 1 + step, n_col)
        slot = chunk if cached else 0
        assemble(chunk, slot)
        part = jnp.dot(dense[slot], feats[...], preferred_element_type=jnp.float32)

        @pl.when(step < n_col - 1)
        def _():
            rs_send[chunk] = part.astype(jnp.bfloat16)
            rs_copy(chunk, col).start()

        @pl.when(step == n_col - 1)
        def _():
            own[...] = part

        return carry

    lax.fori_loop(0, n_col, forward, 0)

    node_scale = jnp.transpose(jnp.broadcast_to(lax.rsqrt(caps[...].astype(jnp.float32)), (half, node)))
    bound = jnp.zeros((1, node), jnp.float32)
    for g in range(bounds_ref.shape[0]):
        bound = bound + jnp.where(groups[...] == g, bounds_ref[g], 0.0)
    bound = jnp.transpose(jnp.broadcast_to(bound, (half, node)))

    for step in range(1, n_col):
        peer = lax.rem(col - step + n_col, n_col)
        rs_copy(peer, peer).wait_recv()
        own[...] += rs_recv[peer].astype(jnp.float32)
    agg[feat] = (own[...] * node_scale).astype(jnp.bfloat16)
    agg_copy = remote(agg.at[feat], agg.at[feat], agg_sem.at[0], agg_sem.at[1], {"feat": other})
    agg_copy.start()
    og_copy.wait()
    agg_copy.wait()

    mine = pl.ds(pl.multiple_of(feat * half, half), half)
    theirs = pl.ds(pl.multiple_of(other * half, half), half)
    agg_0, agg_1 = agg[0], agg[1]

    def activation(columns):
        return jnp.dot(agg_0, weight[:half, columns], preferred_element_type=jnp.float32) + jnp.dot(
            agg_1, weight[half:, columns], preferred_element_type=jnp.float32
        )

    def gated(pre, cotangent):
        sig = 1.0 / (1.0 + jnp.exp(-pre))
        return sig, (cotangent.astype(jnp.float32) * sig * (1.0 + pre * (1.0 - sig))).astype(jnp.bfloat16)

    pre_mine = activation(mine)
    sig_mine, grad_mine = gated(pre_mine, out_grad[...])
    _, grad_theirs = gated(activation(theirs), og_peer[...])
    dims = (((1,), (1,)), ((), ()))
    back = lax.dot_general(grad_mine, weight[mine, mine], dims, preferred_element_type=jnp.float32)
    back += lax.dot_general(grad_theirs, weight[mine, theirs], dims, preferred_element_type=jnp.float32)
    grads[col] = jnp.transpose(back * node_scale).astype(jnp.bfloat16)

    def ag_copy(peer, sender):
        return remote(grads.at[sender], grads.at[sender], ag_ssem.at[peer], ag_rsem.at[sender], {"col": peer})

    for step in range(1, n_col):
        ag_copy(lax.rem(col + step, n_col), col).start()

    out_feat[...] = (pre_mine * sig_mine).astype(jnp.bfloat16)
    feat_out = pltpu.make_async_copy(out_feat, out_feat_hbm, out_sem.at[0])
    feat_out.start()

    def squares(a, b):
        a, b = a.astype(jnp.float32), b.astype(jnp.float32)
        return jnp.sum(a * a + b * b, axis=1, keepdims=True)

    norm = jnp.sqrt(squares(agg_0, agg_1) + 1e-06) * jnp.sqrt(squares(grad_mine, grad_theirs) + 1e-06)
    factor = jnp.minimum(1.0, bound / norm)
    clipped = (factor * grad_mine.astype(jnp.float32)).astype(jnp.bfloat16)
    dims = (((0,), (0,)), ((), ()))
    w_local[:half] = lax.dot_general(agg_0, clipped, dims, preferred_element_type=jnp.float32)
    w_local[half:] = lax.dot_general(agg_1, clipped, dims, preferred_element_type=jnp.float32)

    def w_part(index):
        return w_local.at[pl.ds(pl.multiple_of(index * w_rows, w_rows), w_rows)]

    def wc_copy(dest, sender):
        return remote(w_part(dest), w_col.at[sender], wc_ssem.at[dest], wc_rsem.at[sender], {"col": dest})

    def wr_copy(dest, sender):
        return remote(w_row.at[sender], w_row.at[sender], wr_ssem.at[dest], wr_rsem.at[sender], {"row": dest})

    def wa_copy(dest, sender):
        return remote(w_all.at[sender], w_all.at[sender], wa_ssem.at[dest], wa_rsem.at[sender], {"col": dest})

    for step in range(1, n_col):
        wc_copy(lax.rem(col + step, n_col), col).start()

    def backward(peer):
        slot = peer if cached else 0
        if not cached:
            assemble(peer, slot)
        return jnp.dot(grads[peer], dense[slot], preferred_element_type=jnp.float32)

    acc[...] = backward(col)

    total = w_part(col)[...]
    for step in range(1, n_col):
        peer = lax.rem(col - step + n_col, n_col)
        wc_copy(peer, peer).wait_recv()
        total += w_col[peer]
    w_row[row] = total
    for step in range(1, n_row):
        wr_copy(lax.rem(row + step, n_row), row).start()

    def backward_step(step, carry):
        peer = lax.rem(col - step + n_col, n_col)
        ag_copy(peer, peer).wait_recv()
        acc[...] += backward(peer)
        return carry

    lax.fori_loop(1, n_col - 1, backward_step, 0)

    tail = lax.rem(col + 1, n_col)
    tail_slot = tail if cached else 0
    if not cached:
        assemble(tail, tail_slot)
    ag_copy(tail, tail).wait_recv()

    def fold_rows():
        for step in range(1, n_row):
            peer = lax.rem(row - step + n_row, n_row)
            wr_copy(peer, peer).wait_recv()
        total = w_row[0]
        for index in range(1, n_row):
            total += w_row[index]
        w_all[col] = total
        for step in range(1, n_col):
            wa_copy(lax.rem(col + step, n_col), col).start()

    last = n_row - 1
    pairs = pieces // 2
    lower = row < n_row // 2
    odd = jnp.where(lower, 1, 0)
    mid = jnp.where(lower, n_row // 2 - 1, n_row // 2)
    is_mid = row == mid

    def span(p):
        return pl.ds(pl.multiple_of(p * PIECE, PIECE), PIECE)

    def send_up(p):
        return remote(z_send.at[p], z_left.at[p], z_ssem.at[p], zl_rsem.at[p], {"row": row + 1})

    def send_down(p):
        return remote(z_send.at[p], z_right.at[p], z_ssem.at[p], zr_rsem.at[p], {"row": row - 1})

    def final(p, way):
        spot = grad_input.at[p]
        return remote(spot, spot, fin_ssem.at[way, p], fin_rsem.at[p], {"row": row + 1 if way else row - 1})

    def store(p):
        return pltpu.make_async_copy(grad_input.at[p], grad_input_hbm.at[span(p)], gin_sem.at[p])

    def own_part(p):
        product = jnp.dot(grads[tail], dense[tail_slot, :, span(p)], preferred_element_type=jnp.float32)
        z_sum[...] = jnp.transpose(acc[:, span(p)] + product)

    def add_left(p, when):
        @pl.when(when)
        def _():
            send_up(p).wait_recv()
            z_sum[...] += z_left[p].astype(jnp.float32)

    def add_right(p, when):
        @pl.when(when)
        def _():
            send_down(p).wait_recv()
            z_sum[...] += z_right[p].astype(jnp.float32)

    def pass_on(p, up, down):
        @pl.when(up | down)
        def _():
            z_send[p] = z_sum[...].astype(jnp.bfloat16)

        @pl.when(up)
        def _():
            send_up(p).start()

        @pl.when(down)
        def _():
            send_down(p).start()

    def first_piece(j):
        p = 2 * j + odd
        own_part(p)
        add_left(p, lower & (row > 0))
        add_right(p, (row >= n_row // 2) & (row < last))
        pass_on(p, lower, row >= n_row // 2)

    def second_piece(j):
        p = 2 * j + 1 - odd
        own_part(p)
        add_left(p, (row > 0) & (row <= n_row // 2))
        add_right(p, (row < last) & (row >= n_row // 2 - 1))
        pass_on(p, row < n_row // 2 - 1, row > n_row // 2)

        @pl.when(is_mid)
        def _():
            grad_input[p] = z_sum[...].astype(jnp.bfloat16)

        @pl.when(is_mid & (row < last))
        def _():
            final(p, 1).start()

        @pl.when(is_mid & (row > 0))
        def _():
            final(p, 0).start()

    def finish(p, wait):
        @pl.when(wait)
        def _():
            final(p, 0).wait_recv()

        @pl.when(wait & lower & (row > 0))
        def _():
            final(p, 0).start()

        @pl.when(wait & (row >= n_row // 2) & (row < last))
        def _():
            final(p, 1).start()

        store(p).start()

    def z_step(j, carry):
        @pl.when(j < pairs)
        def _():
            first_piece(j)

        @pl.when((j >= LEAD) & (j < pairs + LEAD))
        def _():
            second_piece(j - LEAD)

        @pl.when(j >= LEAD + LAG)
        def _():
            done = j - LEAD - LAG
            finish(2 * done + odd, row >= 0)
            finish(2 * done + 1 - odd, row != mid)

        return carry

    lax.fori_loop(0, 1, z_step, 0)
    fold_rows()
    lax.fori_loop(1, pairs + LEAD + LAG, z_step, 0)

    for step in range(1, n_col):
        peer = lax.rem(col - step + n_col, n_col)
        wa_copy(peer, peer).wait_recv()
    for index in range(n_col):
        spot = pl.ds(index * w_rows, w_rows)
        grad_weight[spot] = w_all[index] * scale + noise[spot]
    weight_out = pltpu.make_async_copy(grad_weight, grad_weight_hbm, out_sem.at[1])
    weight_out.start()

    for step in range(1, n_col):
        peer = lax.rem(col + step, n_col)
        rs_copy(peer, col).wait_send()
        ag_copy(peer, col).wait_send()
        wc_copy(peer, col).wait_send()
        wa_copy(peer, col).wait_send()
    for step in range(1, n_row):
        wr_copy(lax.rem(row + step, n_row), row).wait_send()

    def drain(j, carry):
        for p, passed, done in (
            (2 * j + odd, row >= 0, row < 0),
            (2 * j + 1 - odd, row != mid, is_mid),
        ):
            @pl.when(passed)
            def _():
                send_up(p).wait_send()

            @pl.when((lower | done) & (row > 0))
            def _():
                final(p, 0).wait_send()

            @pl.when(((row >= n_row // 2) | done) & (row < last))
            def _():
                final(p, 1).wait_send()

            store(p).wait()
        return carry

    lax.fori_loop(0, pairs, drain, 0)
    feat_out.wait()
    weight_out.wait()


def deliver(a_in, b_in, c_in, a_out, b_out, c_out, a_buf, b_buf, c_buf, sems):
    rows = ((a_in, a_buf, a_out), (b_in, b_buf, b_out), (c_in, c_buf, c_out))
    loads = [pltpu.make_async_copy(src, buf, sems.at[0, i]) for i, (src, buf, _) in enumerate(rows)]
    stores = [pltpu.make_async_copy(buf, dst, sems.at[1, i]) for i, (_, buf, dst) in enumerate(rows)]
    for copy in loads:
        copy.start()
    for load, store in zip(loads, stores):
        load.wait()
        store.start()
    for copy in stores:
        copy.wait()


def per_device(
    tile_values, tile_rows, tile_cols, tile_mask, degree_caps, clip_groups,
    clip_bounds, features, weight, out_grad, dp_noise,
):
    tile_vals = tile_values[0, 0]
    slots, blk = tile_vals.shape[0], tile_vals.shape[1]
    node, half = out_grad.shape
    n_col, n_row = lax.axis_size("col"), lax.axis_size("row")
    col_range = features.shape[0]
    row_blocks, col_blocks = node * n_col // blk, col_range // blk
    hid = weight.shape[0]
    pair = jnp.where(tile_mask[0, 0] == 1, tile_rows[0, 0] * col_blocks + tile_cols[0, 0], -1)
    wanted = jnp.arange(row_blocks * col_blocks, dtype=jnp.int32)
    order = jnp.arange(slots, dtype=jnp.int32)
    slot_map = jnp.min(jnp.where(pair[:, None] == wanted[None, :], order[:, None], slots), axis=0)
    cached = row_blocks * col_blocks * blk * blk * 2 <= (20 << 20)
    pieces = col_range // PIECE
    bf16, f32 = jnp.bfloat16, jnp.float32
    vmem, smem = pl.BlockSpec(memory_space=pltpu.VMEM), pl.BlockSpec(memory_space=pltpu.SMEM)
    anywhere = pl.BlockSpec(memory_space=pl.ANY)
    sem = pltpu.SemaphoreType.DMA
    shapes = (
        jax.ShapeDtypeStruct((node, half), bf16),
        jax.ShapeDtypeStruct((hid, half), f32),
        jax.ShapeDtypeStruct((col_range, half), bf16),
    )
    call = pl.pallas_call(
        functools.partial(layer, n_row, n_col, 1.0 / math.sqrt(node * n_col * n_row), cached),
        out_shape=shapes,
        in_specs=[smem, smem] + [anywhere] * 5 + [vmem] * 2,
        out_specs=[anywhere] * 3,
        scratch_shapes=[
            pltpu.VMEM((col_range, half), bf16),
            pltpu.VMEM((hid, hid), bf16),
            pltpu.VMEM((node, half), bf16),
            pltpu.VMEM((hid, half), f32),
            pltpu.VMEM((node, half), bf16),
            pltpu.VMEM((hid, half), f32),
            pltpu.VMEM((pieces, PIECE, half), bf16),
            pltpu.VMEM((slots + 1, blk, blk), bf16),
            pltpu.VMEM((n_col if cached else 1, node, col_range), bf16),
            pltpu.VMEM((n_col, node, half), bf16),
            pltpu.VMEM((n_col, node, half), bf16),
            pltpu.VMEM((node, half), f32),
            pltpu.VMEM((node, half), bf16),
            pltpu.VMEM((2, node, half), bf16),
            pltpu.VMEM((n_col, half, node), bf16),
            pltpu.VMEM((half, col_range), f32),
            pltpu.VMEM((hid, half), f32),
            pltpu.VMEM((n_col, hid // n_col, half), f32),
            pltpu.VMEM((n_row, hid // n_col, half), f32),
            pltpu.VMEM((n_col, hid // n_col, half), f32),
            pltpu.VMEM((pieces, PIECE, half), bf16),
            pltpu.VMEM((pieces, PIECE, half), bf16),
            pltpu.VMEM((pieces, PIECE, half), bf16),
            pltpu.VMEM((PIECE, half), f32),
            sem((LOADS,)), sem((4,)), sem((2,)), sem((pieces,)), sem((2,)), sem((2,)),
            sem((n_col,)), sem((n_col,)), sem((n_col,)), sem((n_col,)),
            sem((n_col,)), sem((n_col,)), sem((n_row,)), sem((n_row,)),
            sem((n_col,)), sem((n_col,)),
            sem((pieces,)), sem((pieces,)), sem((pieces,)), sem((2, pieces)), sem((pieces,)),
        ],
        compiler_params=pltpu.CompilerParams(
            collective_id=0, has_side_effects=True, vmem_limit_bytes=56 << 20
        ),
        name="layer",
    )
    results = call(
        slot_map, clip_bounds, tile_vals, features, weight, out_grad, dp_noise,
        degree_caps[None, :], clip_groups[None, :],
    )
    return pl.pallas_call(
        deliver,
        out_shape=shapes,
        in_specs=[anywhere] * 3,
        out_specs=[anywhere] * 3,
        scratch_shapes=[pltpu.VMEM(x.shape, x.dtype) for x in shapes] + [sem((2, 3))],
        name="deliver",
    )(*results)


def solution(mesh):
    placed = (
        P("row", "col", None, None, None),
        P("row", "col", None),
        P("row", "col", None),
        P("row", "col", None),
        P(("row", "col")),
        P(("row", "col")),
        P(),
        P("col", "feat"),
        P(),
        P(("row", "col"), "feat"),
        P(None, "feat"),
    )
    return jax.shard_map(
        per_device,
        mesh=mesh,
        in_specs=placed,
        out_specs=(P(("row", "col"), "feat"), P(None, "feat"), P("col", "feat")),
        check_vma=False,
    )
```

```python
import functools
import math

import jax
import jax.numpy as jnp
from jax import lax
from jax.experimental import pallas as pl
from jax.experimental.pallas import tpu as pltpu
from jax.sharding import PartitionSpec as P

MESH = pl.DeviceIdType.MESH
PIECE = 256
LEAD = 2
LAG = 3
LOADS = 4


def layer(
    n_row, n_col, scale, cached,
    map_ref, bounds_ref, tiles_hbm, feats_hbm, weight_hbm, og_hbm, noise_hbm, caps, groups,
    out_feat_hbm, grad_weight_hbm, grad_input_hbm,
    feats, weight, out_grad, noise, out_feat, grad_weight, grad_input,
    tiles, dense, rs_send, rs_recv, own, og_peer, agg, grads, acc,
    w_local, w_col, w_row, w_all, z_left, z_right, z_send, z_sum,
    tile_sem, in_sem, out_sem, gin_sem, og_sem, agg_sem, rs_ssem, rs_rsem, ag_ssem, ag_rsem,
    wc_ssem, wc_rsem, wr_ssem, wr_rsem, wa_ssem, wa_rsem,
    z_ssem, zl_rsem, zr_rsem, fin_ssem, fin_rsem,
):
    row, col, feat = lax.axis_index("row"), lax.axis_index("col"), lax.axis_index("feat")
    other = 1 - feat
    slots, blk = tiles_hbm.shape[0], tiles_hbm.shape[1]
    node, half = og_hbm.shape
    col_blocks = feats.shape[0] // blk
    sub = node // blk
    w_rows = w_col.shape[1]
    pieces = z_send.shape[0]

    def remote(src, dst, ssem, rsem, where):
        return pltpu.make_async_remote_copy(
            src_ref=src, dst_ref=dst, send_sem=ssem, recv_sem=rsem,
            device_id=where, device_id_type=MESH,
        )

    count = slots // LOADS
    loads = [
        pltpu.make_async_copy(
            tiles_hbm.at[pl.ds(i * count, count)], tiles.at[pl.ds(i * count, count)], tile_sem.at[i]
        )
        for i in range(LOADS)
    ]
    inputs = [
        pltpu.make_async_copy(src, dst, in_sem.at[i])
        for i, (src, dst) in enumerate(
            ((feats_hbm, feats), (og_hbm, out_grad), (weight_hbm, weight), (noise_hbm, noise))
        )
    ]
    for copy in loads + inputs:
        copy.start()

    barrier = pltpu.get_barrier_semaphore()
    pl.semaphore_signal(barrier, inc=1, device_id={"feat": other}, device_id_type=MESH)
    for step in range(1, n_col):
        pl.semaphore_signal(barrier, inc=1, device_id={"col": lax.rem(col + step, n_col)}, device_id_type=MESH)
    for step in range(1, n_row):
        pl.semaphore_signal(barrier, inc=1, device_id={"row": lax.rem(row + step, n_row)}, device_id_type=MESH)
    tiles[slots] = jnp.zeros((blk, blk), jnp.bfloat16)
    pl.semaphore_wait(barrier, n_col + n_row - 1)

    og_copy = remote(og_hbm, og_peer, og_sem.at[0], og_sem.at[1], {"feat": other})
    for copy in loads + inputs[:1]:
        copy.wait()

    def assemble(chunk, slot):
        for rb in range(sub):
            for cb in range(col_blocks):
                which = map_ref[(chunk * sub + rb) * col_blocks + cb]
                dense[slot, rb * blk:(rb + 1) * blk, cb * blk:(cb + 1) * blk] = tiles[which]

    def rs_copy(dest, sender):
        return remote(rs_send.at[dest], rs_recv.at[sender], rs_ssem.at[dest], rs_rsem.at[sender], {"col": dest})

    def forward(step, carry):
        chunk = lax.rem(col + 1 + step, n_col)
        slot = chunk if cached else 0
        assemble(chunk, slot)
        part = jnp.dot(dense[slot], feats[...], preferred_element_type=jnp.float32)

        @pl.when(step < n_col - 1)
        def _():
            rs_send[chunk] = part.astype(jnp.bfloat16)
            rs_copy(chunk, col).start()

        @pl.when(step == n_col - 1)
        def _():
            own[...] = part

        return carry

    lax.fori_loop(0, n_col, forward, 0)
    og_copy.start()

    node_scale = jnp.transpose(jnp.broadcast_to(lax.rsqrt(caps[...].astype(jnp.float32)), (half, node)))
    bound = jnp.zeros((1, node), jnp.float32)
    for g in range(bounds_ref.shape[0]):
        bound = bound + jnp.where(groups[...] == g, bounds_ref[g], 0.0)
    bound = jnp.transpose(jnp.broadcast_to(bound, (half, node)))

    for step in range(1, n_col):
        peer = lax.rem(col - step + n_col, n_col)
        rs_copy(peer, peer).wait_recv()
        own[...] += rs_recv[peer].astype(jnp.float32)
    agg[feat] = (own[...] * node_scale).astype(jnp.bfloat16)
    agg_copy = remote(agg.at[feat], agg.at[feat], agg_sem.at[0], agg_sem.at[1], {"feat": other})
    agg_copy.start()
    for copy in inputs[1:]:
        copy.wait()
    og_copy.wait()
    agg_copy.wait()

    mine = pl.ds(pl.multiple_of(feat * half, half), half)
    theirs = pl.ds(pl.multiple_of(other * half, half), half)
    agg_0, agg_1 = agg[0], agg[1]

    def activation(columns):
        return jnp.dot(agg_0, weight[:half, columns], preferred_element_type=jnp.float32) + jnp.dot(
            agg_1, weight[half:, columns], preferred_element_type=jnp.float32
        )

    def gated(pre, cotangent):
        sig = 1.0 / (1.0 + jnp.exp(-pre))
        return sig, (cotangent.astype(jnp.float32) * sig * (1.0 + pre * (1.0 - sig))).astype(jnp.bfloat16)

    pre_mine = activation(mine)
    sig_mine, grad_mine = gated(pre_mine, out_grad[...])
    _, grad_theirs = gated(activation(theirs), og_peer[...])
    dims = (((1,), (1,)), ((), ()))
    back = lax.dot_general(grad_mine, weight[mine, mine], dims, preferred_element_type=jnp.float32)
    back += lax.dot_general(grad_theirs, weight[mine, theirs], dims, preferred_element_type=jnp.float32)
    grads[col] = jnp.transpose(back * node_scale).astype(jnp.bfloat16)

    def ag_copy(peer, sender):
        return remote(grads.at[sender], grads.at[sender], ag_ssem.at[peer], ag_rsem.at[sender], {"col": peer})

    for step in range(1, n_col):
        ag_copy(lax.rem(col + step, n_col), col).start()

    out_feat[...] = (pre_mine * sig_mine).astype(jnp.bfloat16)
    feat_out = pltpu.make_async_copy(out_feat, out_feat_hbm, out_sem.at[0])
    feat_out.start()

    def squares(a, b):
        a, b = a.astype(jnp.float32), b.astype(jnp.float32)
        return jnp.sum(a * a + b * b, axis=1, keepdims=True)

    norm = jnp.sqrt(squares(agg_0, agg_1) + 1e-06) * jnp.sqrt(squares(grad_mine, grad_theirs) + 1e-06)
    factor = jnp.minimum(1.0, bound / norm)
    clipped = (factor * grad_mine.astype(jnp.float32)).astype(jnp.bfloat16)
    dims = (((0,), (0,)), ((), ()))
    w_local[:half] = lax.dot_general(agg_0, clipped, dims, preferred_element_type=jnp.float32)
    w_local[half:] = lax.dot_general(agg_1, clipped, dims, preferred_element_type=jnp.float32)

    def w_part(index):
        return w_local.at[pl.ds(pl.multiple_of(index * w_rows, w_rows), w_rows)]

    def wc_copy(dest, sender):
        return remote(w_part(dest), w_col.at[sender], wc_ssem.at[dest], wc_rsem.at[sender], {"col": dest})

    def wr_copy(dest, sender):
        return remote(w_row.at[sender], w_row.at[sender], wr_ssem.at[dest], wr_rsem.at[sender], {"row": dest})

    def wa_copy(dest, sender):
        return remote(w_all.at[sender], w_all.at[sender], wa_ssem.at[dest], wa_rsem.at[sender], {"col": dest})

    for step in range(1, n_col):
        wc_copy(lax.rem(col + step, n_col), col).start()

    def backward(peer):
        slot = peer if cached else 0
        if not cached:
            assemble(peer, slot)
        return jnp.dot(grads[peer], dense[slot], preferred_element_type=jnp.float32)

    acc[...] = backward(col)

    total = w_part(col)[...]
    for step in range(1, n_col):
        peer = lax.rem(col - step + n_col, n_col)
        wc_copy(peer, peer).wait_recv()
        total += w_col[peer]
    w_row[row] = total
    for step in range(1, n_row):
        wr_copy(lax.rem(row + step, n_row), row).start()

    def backward_step(step, carry):
        peer = lax.rem(col - step + n_col, n_col)
        ag_copy(peer, peer).wait_recv()
        acc[...] += backward(peer)
        return carry

    lax.fori_loop(1, n_col - 1, backward_step, 0)

    tail = lax.rem(col + 1, n_col)
    tail_slot = tail if cached else 0
    if not cached:
        assemble(tail, tail_slot)
    ag_copy(tail, tail).wait_recv()

    def fold_rows():
        for step in range(1, n_row):
            peer = lax.rem(row - step + n_row, n_row)
            wr_copy(peer, peer).wait_recv()
        total = w_row[0]
        for index in range(1, n_row):
            total += w_row[index]
        w_all[col] = total
        for step in range(1, n_col):
            wa_copy(lax.rem(col + step, n_col), col).start()

    last = n_row - 1
    pairs = pieces // 2
    lower = row < n_row // 2
    odd = jnp.where(lower, 1, 0)
    mid = jnp.where(lower, n_row // 2 - 1, n_row // 2)
    is_mid = row == mid

    def span(p):
        return pl.ds(pl.multiple_of(p * PIECE, PIECE), PIECE)

    def send_up(p):
        return remote(z_send.at[p], z_left.at[p], z_ssem.at[p], zl_rsem.at[p], {"row": row + 1})

    def send_down(p):
        return remote(z_send.at[p], z_right.at[p], z_ssem.at[p], zr_rsem.at[p], {"row": row - 1})

    def final(p, way):
        spot = grad_input.at[p]
        return remote(spot, spot, fin_ssem.at[way, p], fin_rsem.at[p], {"row": row + 1 if way else row - 1})

    def store(p):
        return pltpu.make_async_copy(grad_input.at[p], grad_input_hbm.at[span(p)], gin_sem.at[p])

    def own_part(p):
        product = jnp.dot(grads[tail], dense[tail_slot, :, span(p)], preferred_element_type=jnp.float32)
        z_sum[...] = jnp.transpose(acc[:, span(p)] + product)

    def add_left(p, when):
        @pl.when(when)
        def _():
            send_up(p).wait_recv()
            z_sum[...] += z_left[p].astype(jnp.float32)

    def add_right(p, when):
        @pl.when(when)
        def _():
            send_down(p).wait_recv()
            z_sum[...] += z_right[p].astype(jnp.float32)

    def pass_on(p, up, down):
        @pl.when(up | down)
        def _():
            z_send[p] = z_sum[...].astype(jnp.bfloat16)

        @pl.when(up)
        def _():
            send_up(p).start()

        @pl.when(down)
        def _():
            send_down(p).start()

    def first_piece(j):
        p = 2 * j + odd
        own_part(p)
        add_left(p, lower & (row > 0))
        add_right(p, (row >= n_row // 2) & (row < last))
        pass_on(p, lower, row >= n_row // 2)

    def second_piece(j):
        p = 2 * j + 1 - odd
        own_part(p)
        add_left(p, (row > 0) & (row <= n_row // 2))
        add_right(p, (row < last) & (row >= n_row // 2 - 1))
        pass_on(p, row < n_row // 2 - 1, row > n_row // 2)

        @pl.when(is_mid)
        def _():
            grad_input[p] = z_sum[...].astype(jnp.bfloat16)

        @pl.when(is_mid & (row < last))
        def _():
            final(p, 1).start()

        @pl.when(is_mid & (row > 0))
        def _():
            final(p, 0).start()

    def finish(p, wait):
        @pl.when(wait)
        def _():
            final(p, 0).wait_recv()

        @pl.when(wait & lower & (row > 0))
        def _():
            final(p, 0).start()

        @pl.when(wait & (row >= n_row // 2) & (row < last))
        def _():
            final(p, 1).start()

        store(p).start()

    def z_step(j, carry):
        @pl.when(j < pairs)
        def _():
            first_piece(j)

        @pl.when((j >= LEAD) & (j < pairs + LEAD))
        def _():
            second_piece(j - LEAD)

        @pl.when(j >= LEAD + LAG)
        def _():
            done = j - LEAD - LAG
            finish(2 * done + odd, row >= 0)
            finish(2 * done + 1 - odd, row != mid)

        return carry

    lax.fori_loop(0, 1, z_step, 0)
    fold_rows()
    lax.fori_loop(1, pairs + LEAD + LAG, z_step, 0)

    for step in range(1, n_col):
        peer = lax.rem(col - step + n_col, n_col)
        wa_copy(peer, peer).wait_recv()
    for index in range(n_col):
        spot = pl.ds(index * w_rows, w_rows)
        grad_weight[spot] = w_all[index] * scale + noise[spot]
    weight_out = pltpu.make_async_copy(grad_weight, grad_weight_hbm, out_sem.at[1])
    weight_out.start()

    for step in range(1, n_col):
        peer = lax.rem(col + step, n_col)
        rs_copy(peer, col).wait_send()
        ag_copy(peer, col).wait_send()
        wc_copy(peer, col).wait_send()
        wa_copy(peer, col).wait_send()
    for step in range(1, n_row):
        wr_copy(lax.rem(row + step, n_row), row).wait_send()

    def drain(j, carry):
        for p, passed, done in (
            (2 * j + odd, row >= 0, row < 0),
            (2 * j + 1 - odd, row != mid, is_mid),
        ):
            @pl.when(passed)
            def _():
                send_up(p).wait_send()

            @pl.when((lower | done) & (row > 0))
            def _():
                final(p, 0).wait_send()

            @pl.when(((row >= n_row // 2) | done) & (row < last))
            def _():
                final(p, 1).wait_send()

            store(p).wait()
        return carry

    lax.fori_loop(0, pairs, drain, 0)
    feat_out.wait()
    weight_out.wait()


def deliver(a_in, b_in, c_in, a_out, b_out, c_out, a_buf, b_buf, c_buf, sems):
    rows = ((a_in, a_buf, a_out), (b_in, b_buf, b_out), (c_in, c_buf, c_out))
    loads = [pltpu.make_async_copy(src, buf, sems.at[0, i]) for i, (src, buf, _) in enumerate(rows)]
    stores = [pltpu.make_async_copy(buf, dst, sems.at[1, i]) for i, (_, buf, dst) in enumerate(rows)]
    for copy in loads:
        copy.start()
    for load, store in zip(loads, stores):
        load.wait()
        store.start()
    for copy in stores:
        copy.wait()


def per_device(
    tile_values, tile_rows, tile_cols, tile_mask, degree_caps, clip_groups,
    clip_bounds, features, weight, out_grad, dp_noise,
):
    tile_vals = tile_values[0, 0]
    slots, blk = tile_vals.shape[0], tile_vals.shape[1]
    node, half = out_grad.shape
    n_col, n_row = lax.axis_size("col"), lax.axis_size("row")
    col_range = features.shape[0]
    row_blocks, col_blocks = node * n_col // blk, col_range // blk
    hid = weight.shape[0]
    pair = jnp.where(tile_mask[0, 0] == 1, tile_rows[0, 0] * col_blocks + tile_cols[0, 0], -1)
    wanted = jnp.arange(row_blocks * col_blocks, dtype=jnp.int32)
    order = jnp.arange(slots, dtype=jnp.int32)
    slot_map = jnp.min(jnp.where(pair[:, None] == wanted[None, :], order[:, None], slots), axis=0)
    cached = row_blocks * col_blocks * blk * blk * 2 <= (20 << 20)
    pieces = col_range // PIECE
    bf16, f32 = jnp.bfloat16, jnp.float32
    vmem, smem = pl.BlockSpec(memory_space=pltpu.VMEM), pl.BlockSpec(memory_space=pltpu.SMEM)
    anywhere = pl.BlockSpec(memory_space=pl.ANY)
    sem = pltpu.SemaphoreType.DMA
    shapes = (
        jax.ShapeDtypeStruct((node, half), bf16),
        jax.ShapeDtypeStruct((hid, half), f32),
        jax.ShapeDtypeStruct((col_range, half), bf16),
    )
    call = pl.pallas_call(
        functools.partial(layer, n_row, n_col, 1.0 / math.sqrt(node * n_col * n_row), cached),
        out_shape=shapes,
        in_specs=[smem, smem] + [anywhere] * 5 + [vmem] * 2,
        out_specs=[anywhere] * 3,
        scratch_shapes=[
            pltpu.VMEM((col_range, half), bf16),
            pltpu.VMEM((hid, hid), bf16),
            pltpu.VMEM((node, half), bf16),
            pltpu.VMEM((hid, half), f32),
            pltpu.VMEM((node, half), bf16),
            pltpu.VMEM((hid, half), f32),
            pltpu.VMEM((pieces, PIECE, half), bf16),
            pltpu.VMEM((slots + 1, blk, blk), bf16),
            pltpu.VMEM((n_col if cached else 1, node, col_range), bf16),
            pltpu.VMEM((n_col, node, half), bf16),
            pltpu.VMEM((n_col, node, half), bf16),
            pltpu.VMEM((node, half), f32),
            pltpu.VMEM((node, half), bf16),
            pltpu.VMEM((2, node, half), bf16),
            pltpu.VMEM((n_col, half, node), bf16),
            pltpu.VMEM((half, col_range), f32),
            pltpu.VMEM((hid, half), f32),
            pltpu.VMEM((n_col, hid // n_col, half), f32),
            pltpu.VMEM((n_row, hid // n_col, half), f32),
            pltpu.VMEM((n_col, hid // n_col, half), f32),
            pltpu.VMEM((pieces, PIECE, half), bf16),
            pltpu.VMEM((pieces, PIECE, half), bf16),
            pltpu.VMEM((pieces, PIECE, half), bf16),
            pltpu.VMEM((PIECE, half), f32),
            sem((LOADS,)), sem((4,)), sem((2,)), sem((pieces,)), sem((2,)), sem((2,)),
            sem((n_col,)), sem((n_col,)), sem((n_col,)), sem((n_col,)),
            sem((n_col,)), sem((n_col,)), sem((n_row,)), sem((n_row,)),
            sem((n_col,)), sem((n_col,)),
            sem((pieces,)), sem((pieces,)), sem((pieces,)), sem((2, pieces)), sem((pieces,)),
        ],
        compiler_params=pltpu.CompilerParams(
            collective_id=0, has_side_effects=True, vmem_limit_bytes=56 << 20
        ),
        name="layer",
    )
    results = call(
        slot_map, clip_bounds, tile_vals, features, weight, out_grad, dp_noise,
        degree_caps[None, :], clip_groups[None, :],
    )
    return pl.pallas_call(
        deliver,
        out_shape=shapes,
        in_specs=[anywhere] * 3,
        out_specs=[anywhere] * 3,
        scratch_shapes=[pltpu.VMEM(x.shape, x.dtype) for x in shapes] + [sem((2, 3))],
        name="deliver",
    )(*results)


def solution(mesh):
    placed = (
        P("row", "col", None, None, None),
        P("row", "col", None),
        P("row", "col", None),
        P("row", "col", None),
        P(("row", "col")),
        P(("row", "col")),
        P(),
        P("col", "feat"),
        P(),
        P(("row", "col"), "feat"),
        P(None, "feat"),
    )
    return jax.shard_map(
        per_device,
        mesh=mesh,
        in_specs=placed,
        out_specs=(P(("row", "col"), "feat"), P(None, "feat"), P("col", "feat")),
        check_vma=False,
    )
```
